32 devices in a mesh: fsdp: 4 (over z), head: 4 (over y, x), tensor: 2 (over core).
Axes of the slice: x: 2, y: 2, z: 4, core: 2. Of those that a mesh axis runs over, the one named last changes fastest.
Arguments:
- tokens: bfloat16 [8192, 2048], P(('fsdp', 'head', 'tensor')), may hold values from -6 to 6
- lengths: int32 [4, 2], P('fsdp'), may hold values from 0 to 2048, as said below
- attention_gain: float32 [2048], replicated, may hold values from 0.5 to 1.5
- query_weight: bfloat16 [2048, 8, 2, 128], P('fsdp', 'head', 'tensor'), may hold values from -0.1875 to 0.1875
- key_weight: bfloat16 [2048, 8, 2, 128], P('fsdp', 'head', 'tensor'), may hold values from -0.1875 to 0.1875
- value_weight: bfloat16 [2048, 8, 256], P('fsdp', 'head', 'tensor'), may hold values from -0.125 to 0.125
- output_weight: bfloat16 [8, 256, 2048], P('head', 'tensor', 'fsdp'), may hold values from -0.125 to 0.125
- lambda_vectors: float32 [8, 4, 128], replicated, may hold values from -0.9 to 0.9
- head_gain: float32 [8, 256], replicated, may hold values from 0.5 to 1.5
- feedforward_gain: float32 [2048], replicated, may hold values from 0.5 to 1.5
- gate_weight: bfloat16 [2048, 5632], P('fsdp', ('head', 'tensor')), may hold values from -0.125 to 0.125
- up_weight: bfloat16 [2048, 5632], P('fsdp', ('head', 'tensor')), may hold values from -0.125 to 0.125
- down_weight: bfloat16 [5632, 2048], P(('head', 'tensor'), 'fsdp'), may hold values from -0.078125 to 0.078125
- cotangent: bfloat16 [8192, 2048], P(('fsdp', 'head', 'tensor')), may hold values from -6 to 6
Outputs:
- block_output: bfloat16 [8192, 2048], P(('fsdp', 'head', 'tensor'))
- tokens_grad: float32 [8192, 2048], P(('fsdp', 'head', 'tensor'))
- attention_gain_grad: float32 [2048], replicated
- query_weight_grad: float32 [2048, 8, 2, 128], P('fsdp', 'head', 'tensor')
- key_weight_grad: float32 [2048, 8, 2, 128], P('fsdp', 'head', 'tensor')
- value_weight_grad: float32 [2048, 8, 256], P('fsdp', 'head', 'tensor')
- output_weight_grad: float32 [8, 256, 2048], P('head', 'tensor', 'fsdp')
- lambda_vectors_grad: float32 [8, 4, 128], replicated
- head_gain_grad: float32 [8, 256], replicated
- feedforward_gain_grad: float32 [2048], replicated
- gate_weight_grad: float32 [2048, 5632], P('fsdp', ('head', 'tensor'))
- up_weight_grad: float32 [2048, 5632], P('fsdp', ('head', 'tensor'))
- down_weight_grad: float32 [5632, 2048], P(('head', 'tensor'), 'fsdp')
The draws below stay inside these ranges and needn't reach their ends.
Inputs may be any that keep to these rules, and one draw needn't show every extreme that they name: Each row of 2048 slots holds one or two sequences packed from its start, given by its two lengths in order (the second 0 where there is one); every sequence has 512 tokens or more, together they take 5 * 256 slots or more of the row, and the slots after them are padding; some row holds a single sequence of 2048 tokens.
All inputs are finite; a program needn't handle non-finite values.
Results may differ from the reference program's by a relative error of at most 0.019.
Values may be sent and summed in bfloat16 or wider, within the bound.
No kernel may reach another device: no remote copies, remote signals or barrier semaphores. Data moves between devices by JAX's collectives and lax.ppermute only.
A program may use at most 320 MiB of HBM per device.

```python
import jax
import jax.numpy as jnp
from jax import lax

D = 2048
H = 8
E = 128
V = 256
FF = 5632
SLOTS = 2048
SEQ_MIN = 512
ROWS = 4
TOKENS = 8192


def draw_lengths(key, part):
    total_key, split_key, choice_key, full_key = jax.random.split(key, 4)
    row_index = jnp.arange(ROWS, dtype=jnp.int32)
    totals = jax.random.randint(total_key, (ROWS,), SLOTS * 5 // 8, SLOTS + 1)
    full_row = jax.random.randint(full_key, (), 0, ROWS)
    totals = jnp.where(row_index == full_row, SLOTS, totals)
    wanted = jax.random.randint(choice_key, (ROWS,), 0, 2)
    upper = jnp.maximum(totals - SEQ_MIN + 1, SEQ_MIN + 1)
    first_try = jax.random.randint(split_key, (ROWS,), SEQ_MIN, upper)
    splitting = (wanted == 1) & (totals >= 2 * SEQ_MIN) & (row_index != full_row)
    first_length = jnp.where(splitting, first_try, totals)
    second_length = jnp.where(splitting, totals - first_try, 0)
    return jnp.stack([first_length, second_length], axis=1).astype(jnp.int32)


def block_scale(own_key, dims, pieces, least, top_value):
    def one(axis_at, blocks):
        steps = jax.random.uniform(jax.random.fold_in(jax.random.fold_in(own_key, 6), axis_at), (blocks,), jnp.float32, least / len(pieces), top_value / len(pieces))
        return jnp.repeat(jnp.exp(steps), dims[axis_at] // blocks).reshape((-1,) + (1,) * (len(dims) - axis_at - 1))

    factor_of = one(*pieces[0])
    for cut in pieces[1:]:
        factor_of = factor_of * one(*cut)
    return factor_of


def noise(key, shape, spread, limit, shards=(), held_as=jnp.bfloat16):
    level = block_scale(key, shape, shards, -0.22, 0.18) if shards else 1.0
    drawn = jax.random.normal(key, shape, jnp.float32) * spread * level
    return jnp.minimum(jnp.maximum(drawn, -limit), limit).astype(held_as)


def setup_inputs(seed: int = 0) -> dict:
    keys = jax.random.split(jax.random.key(seed), 15)
    return {
        "tokens": noise(keys[0], (TOKENS, D), 1.0, 6.0, ((0, 32),)),
        "lengths": draw_lengths(jax.random.fold_in(keys[14], 71), 0),
        "attention_gain": jnp.clip(1.0 + 0.1 * jax.random.normal(keys[2], (D,), jnp.float32), 0.5, 1.5),
        "query_weight": noise(keys[3], (D, H, 2, E), (D // 2) ** -0.5, 0.1875, ((0, 4), (1, 4), (2, 2))),
        "key_weight": noise(keys[4], (D, H, 2, E), (D // 2) ** -0.5, 0.1875, ((0, 4), (1, 4), (2, 2))),
        "value_weight": noise(keys[5], (D, H, V), D ** -0.5, 0.125, ((0, 4), (1, 4), (2, 2))),
        "output_weight": noise(keys[6], (H, V, D), (H * V) ** -0.5, 0.125, ((0, 4), (1, 2), (2, 4))),
        "lambda_vectors": noise(keys[7], (H, 4, E), 0.15, 0.9, (), jnp.float32),
        "head_gain": jnp.clip(1.0 + 0.1 * jax.random.normal(keys[8], (H, V), jnp.float32), 0.5, 1.5),
        "feedforward_gain": jnp.clip(1.0 + 0.1 * jax.random.normal(keys[9], (D,), jnp.float32), 0.5, 1.5),
        "gate_weight": noise(keys[10], (D, FF), D ** -0.5, 0.125, ((0, 4), (1, 8))),
        "up_weight": noise(keys[11], (D, FF), D ** -0.5, 0.125, ((0, 4), (1, 8))),
        "down_weight": noise(keys[12], (FF, D), FF ** -0.5, 0.078125, ((0, 8), (1, 4))),
        "cotangent": noise(keys[13], (TOKENS, D), 1.0, 6.0, ((0, 32),)),
    }


@jax.custom_vjp
def low(v):
    return lax.optimization_barrier(v.astype(jnp.bfloat16)).astype(jnp.float32)

@jax.custom_vjp
def low_back(v):
    return v

def low_keep(v):
    return (low(v), None)

def low_pass(kept, grad):
    return (grad,)

def back_keep(v):
    return (v, None)

def back_low(kept, grad):
    return (low(grad),)
low.defvjp(low_keep, low_pass)
low_back.defvjp(back_keep, back_low)
lambda_base = 0.2

def product(left_side, right_side):
    return jnp.dot(left_side, right_side, precision=lax.Precision.HIGHEST)

def slot_layout(row_lengths):
    slot_index = jnp.arange(SLOTS, dtype=jnp.int32)
    first_end = row_lengths[:, 0:1]
    second_end = first_end + row_lengths[:, 1:2]
    segment = (slot_index[None, :] >= first_end).astype(jnp.int32) + (slot_index[None, :] >= second_end).astype(jnp.int32)
    starts = jnp.where(segment == 0, 0, jnp.where(segment == 1, first_end, second_end)).astype(jnp.int32)
    return (segment, slot_index[None, :] - starts)

def rope_tables(positions, qk_width):
    half_width = qk_width // 2
    frequency = 10000.0 ** (-jnp.arange(half_width, dtype=jnp.float32) / half_width)
    angles = positions.astype(jnp.float32)[:, None] * frequency[None, :]
    return (jnp.cos(angles), jnp.sin(angles))

def rotate(values, cosine_table, sine_table):
    half_width = values.shape[-1] // 2
    first_half = values[..., :half_width]
    second_half = values[..., half_width:]
    cosine_wide = cosine_table[:, None, :]
    sine_wide = sine_table[:, None, :]
    return jnp.concatenate([first_half * cosine_wide - second_half * sine_wide, second_half * cosine_wide + first_half * sine_wide], axis=-1)

def block_row(row_values, row_lengths, weights):
    attention_gain, query_weight, key_weight, value_weight, output_weight, lambda_vectors, head_gain, feedforward_gain, gate_weight, up_weight, down_weight = weights
    heads = query_weight.shape[1]
    qk_width = query_weight.shape[3]
    segment, positions = slot_layout(row_lengths[None, :])
    segment = segment[0]
    positions = positions[0]
    valid = (segment < 2).astype(jnp.float32)[:, None]
    slot_index = jnp.arange(SLOTS, dtype=jnp.int32)
    allowed = (segment[:, None] == segment[None, :]) & (slot_index[None, :] <= slot_index[:, None])
    attention_scale = lax.rsqrt(lax.optimization_barrier(jnp.mean(row_values * row_values, axis=-1, keepdims=True)) + 1e-06)
    normed = low(row_values * attention_scale * attention_gain)
    cosine_table, sine_table = rope_tables(positions, qk_width)
    query_pre = low_back(product(normed, query_weight.reshape(D, -1))).reshape(SLOTS, heads * 2, qk_width)
    queries = low(rotate(query_pre, cosine_table, sine_table) * qk_width ** (-0.5)).reshape(SLOTS, heads, 2, qk_width)
    key_pre = low_back(product(normed, key_weight.reshape(D, -1))).reshape(SLOTS, heads * 2, qk_width)
    keys_all = low(rotate(key_pre, cosine_table, sine_table)).reshape(SLOTS, heads, 2, qk_width)
    values_all = low(low_back(product(normed, value_weight.reshape(D, -1)))).reshape(SLOTS, heads, -1)
    scores = low_back(jnp.einsum('qhme,khme->hmqk', queries, keys_all, precision=lax.Precision.HIGHEST))
    masked = jnp.where(allowed[None, None], scores, -1e+30)
    probability = low(jax.nn.softmax(masked, axis=-1))
    maps_out = low_back(jnp.einsum('hmqk,khv->qhmv', probability, values_all, precision=lax.Precision.HIGHEST))
    first_dot = lax.optimization_barrier(jnp.sum(lambda_vectors[:, 0] * lambda_vectors[:, 1], axis=-1))
    second_dot = lax.optimization_barrier(jnp.sum(lambda_vectors[:, 2] * lambda_vectors[:, 3], axis=-1))
    lambda_value = jnp.exp(first_dot) - jnp.exp(second_dot) + lambda_base
    mixed = maps_out[:, :, 0] - lambda_value[None, :, None] * maps_out[:, :, 1]
    head_scale = lax.rsqrt(lax.optimization_barrier(jnp.mean(mixed * mixed, axis=-1, keepdims=True)) + 1e-05)
    head_out = low(mixed * head_scale * head_gain * (1.0 - lambda_base))
    attention_out = low_back(product(head_out.reshape(SLOTS, -1), output_weight.reshape(-1, D)))
    residual = row_values + attention_out
    ffn_scale = lax.rsqrt(lax.optimization_barrier(jnp.mean(residual * residual, axis=-1, keepdims=True)) + 1e-06)
    ffn_in = low(residual * ffn_scale * feedforward_gain)
    gate_pre = low_back(product(ffn_in, gate_weight))
    upward = low_back(product(ffn_in, up_weight))
    hidden = low(jax.nn.silu(gate_pre) * upward)
    ffn_out = low_back(product(hidden, down_weight))
    return valid * (residual + ffn_out)

def reference(tokens, lengths, attention_gain, query_weight, key_weight, value_weight, output_weight, lambda_vectors, head_gain, feedforward_gain, gate_weight, up_weight, down_weight, cotangent):
    params = tuple((weight.astype(jnp.float32) for weight in (attention_gain, query_weight, key_weight, value_weight, output_weight, lambda_vectors, head_gain, feedforward_gain, gate_weight, up_weight, down_weight)))
    rows_in = tokens.astype(jnp.float32).reshape(ROWS, SLOTS, D)

    def forward(rows_values, weights):

        def run_row(item):
            return jax.checkpoint(block_row)(item[0], item[1], weights)
        return lax.map(run_row, (rows_values, lengths))
    result, pullback = jax.vjp(forward, rows_in, params)
    rows_grad, grads = pullback(cotangent.astype(jnp.float32).reshape(ROWS, SLOTS, D))
    return (result.reshape(TOKENS, D).astype(jnp.bfloat16), rows_grad.reshape(TOKENS, D), grads[0], grads[1], grads[2], grads[3], grads[4], grads[5], grads[6], grads[7], grads[8], grads[9], grads[10])
```

```python
import jax
import jax.numpy as jnp
from jax import lax
from jax.experimental import pallas as pl
from jax.experimental.pallas import tpu as pltpu
from jax.sharding import PartitionSpec as P


SLOTS = 2048
lambda_base = 0.2
block_limit = 512
bf16 = jnp.bfloat16
f32 = jnp.float32


def slot_layout(row_lengths):
    slot_index = jnp.arange(SLOTS, dtype=jnp.int32)
    first_end = row_lengths[:, 0:1]
    second_end = first_end + row_lengths[:, 1:2]
    segment = (slot_index[None, :] >= first_end).astype(jnp.int32) + (
        slot_index[None, :] >= second_end
    ).astype(jnp.int32)
    starts = jnp.where(segment == 0, 0, jnp.where(segment == 1, first_end, second_end))
    return (segment, slot_index[None, :] - starts)


def rope_tables(positions, qk_width):
    half_width = qk_width // 2
    frequency = 10000.0 ** (-jnp.arange(half_width, dtype=f32) / half_width)
    angles = positions.astype(f32)[:, None] * frequency[None, :]
    cosine, sine = jnp.cos(angles), jnp.sin(angles)
    return (
        jnp.concatenate([cosine, cosine], axis=1),
        jnp.concatenate([-sine, sine], axis=1),
    )


def dot(left_side, right_side):
    return jnp.dot(left_side, right_side, preferred_element_type=f32)


def contract_first(left_side, right_side):
    return lax.dot_general(
        left_side, right_side, (((0,), (0,)), ((), ())), preferred_element_type=f32
    )


def contract_last(left_side, right_side):
    return lax.dot_general(
        left_side, right_side, (((1,), (1,)), ((), ())), preferred_element_type=f32
    )


def flip(values, axis, mask):
    size = lax.axis_size(axis)
    return lax.ppermute(values, axis, [(i, i ^ mask) for i in range(size)])


def after(values, *others):
    return lax.optimization_barrier((values, *others))[0]


def gather_rows(own):
    half = own.shape[0] // 2
    near = flip(own, "head", 1)
    far = flip(own, "head", 2)
    top = flip(far[:half], "head", 1)
    bottom = flip(near[half:], "head", 2)
    blocks = [own, near, far, top, bottom]
    others = [flip(block, "tensor", 1) for block in blocks]
    order = []
    for index in range(3):
        order += [blocks[index], others[index]]
    order += [blocks[3], blocks[4], others[3], others[4]]
    return jnp.concatenate(order, axis=0)


def scatter_rows(part_of):
    sums = {}
    for index in (3, 1, 2, 0):
        part = part_of(index)
        rows = part.shape[0] // 2
        passed = flip(part[rows:].astype(bf16), "tensor", 1)
        sums[index] = part[:rows].astype(f32) + passed.astype(f32)
    half = rows // 2
    diagonal = sums[3].astype(bf16)
    top = flip(diagonal[:half], "head", 1).astype(f32)
    bottom = flip(diagonal[half:], "head", 2).astype(f32)
    near_top = flip(sums[1][:half].astype(bf16), "head", 1)
    far_bottom = flip(sums[2][half:].astype(bf16), "head", 2)
    near_bottom = flip((sums[1][half:] + bottom).astype(bf16), "head", 1)
    far_top = flip((sums[2][:half] + top).astype(bf16), "head", 2)
    near = jnp.concatenate([near_top, near_bottom], axis=0).astype(f32)
    far = jnp.concatenate([far_top, far_bottom], axis=0).astype(f32)
    return sums[0] + near + far


class Chain:
    def __init__(self, depth):
        self.depth = depth
        self.done = []

    def step(self, values):
        if len(self.done) >= self.depth:
            values = after(values, self.done[-self.depth])
        size = lax.axis_size("fsdp")
        moved = lax.ppermute(values, "fsdp", [(i, (i + 1) % size) for i in range(size)])
        self.done.append(moved)
        return moved


def ring_gather(chain, shard, axis):
    size = lax.axis_size("fsdp")
    place = lax.axis_index("fsdp")
    width = shard.shape[axis]
    shape = list(shard.shape)
    shape[axis] = width * size
    full = jnp.zeros(shape, shard.dtype)
    moving = shard
    for hop in range(size):
        if hop:
            moving = chain.step(moving)
        start = jnp.remainder(place - hop, size) * width
        full = lax.dynamic_update_slice_in_dim(full, moving, start, axis)
    return full


def ring_scatter(chain, full, axis):
    size = lax.axis_size("fsdp")
    place = lax.axis_index("fsdp")
    width = full.shape[axis] // size

    def chunk(hop):
        start = jnp.remainder(place - 1 - hop, size) * width
        return lax.dynamic_slice_in_dim(full, start, width, axis)

    total = chunk(0).astype(bf16)
    for hop in range(1, size):
        total = chain.step(total).astype(f32) + chunk(hop).astype(f32)
        if hop < size - 1:
            total = total.astype(bf16)
    return total


def total_over(values, axes):
    for axis in axes:
        mask = 1
        while mask < lax.axis_size(axis):
            values = values + flip(values, axis, mask)
            mask *= 2
    return values


def spin(values, cosine, sine):
    return values * cosine + pltpu.roll(values, values.shape[1] // 2, 1) * sine


def rope_blocks(rank, pre, cosine, sine, heads, width, blocks):
    slots, full = pre.shape
    rows = slots // blocks
    part = full // 3

    def kernel(rank_ref, pre_ref, cosine_ref, sine_ref, q_ref, k_ref, v_ref):
        cos, sin = cosine_ref[...], sine_ref[...]
        for head in range(heads):
            at = head * width
            q_ref[:, at : at + width] = (
                spin(pre_ref[:, at : at + width], cos, sin) * width ** (-0.5)
            ).astype(bf16)
            k_ref[:, at : at + width] = spin(
                pre_ref[:, part + at : part + at + width], cos, sin
            ).astype(bf16)
        v_ref[...] = pre_ref[:, 2 * part :].astype(bf16)

    straight = lambda i, rank_ref: (i, 0)
    return pl.pallas_call(
        kernel,
        grid_spec=pltpu.PrefetchScalarGridSpec(
            num_scalar_prefetch=1,
            grid=(blocks,),
            in_specs=[
                pl.BlockSpec((rows, full), lambda i, rank_ref: (i ^ rank_ref[0], 0)),
                pl.BlockSpec((rows, width), straight),
                pl.BlockSpec((rows, width), straight),
            ],
            out_specs=[pl.BlockSpec((rows, part), straight)] * 3,
        ),
        out_shape=[jax.ShapeDtypeStruct((slots, part), bf16)] * 3,
        name="rope",
    )(rank, pre, cosine, sine)


def rope_back_blocks(rank, query_grad, key_grad, value_grad, cosine, sine, heads, width, blocks):
    slots, part = query_grad.shape
    rows = slots // blocks

    def kernel(rank_ref, q_ref, k_ref, v_ref, cosine_ref, sine_ref, out_ref):
        cos, sin = cosine_ref[...], -sine_ref[...]
        for head in range(heads):
            at = head * width
            out_ref[:, at : at + width] = spin(
                q_ref[:, at : at + width] * width ** (-0.5), cos, sin
            ).astype(bf16)
            out_ref[:, part + at : part + at + width] = spin(
                k_ref[:, at : at + width], cos, sin
            ).astype(bf16)
        out_ref[:, 2 * part :] = v_ref[...].astype(bf16)

    straight = lambda i, rank_ref: (i, 0)
    return pl.pallas_call(
        kernel,
        grid_spec=pltpu.PrefetchScalarGridSpec(
            num_scalar_prefetch=1,
            grid=(blocks,),
            in_specs=[pl.BlockSpec((rows, part), straight)] * 3
            + [pl.BlockSpec((rows, width), straight)] * 2,
            out_specs=pl.BlockSpec((rows, 3 * part), lambda i, rank_ref: (i ^ rank_ref[0], 0)),
        ),
        out_shape=jax.ShapeDtypeStruct((slots, 3 * part), bf16),
        name="rope_back",
    )(rank, query_grad, key_grad, value_grad, cosine, sine)


def reorder(rank, values, blocks):
    slots, width = values.shape
    rows = slots // blocks

    def kernel(rank_ref, in_ref, out_ref):
        out_ref[...] = in_ref[...]

    return pl.pallas_call(
        kernel,
        grid_spec=pltpu.PrefetchScalarGridSpec(
            num_scalar_prefetch=1,
            grid=(blocks,),
            in_specs=[pl.BlockSpec((rows, width), lambda i, rank_ref: (i ^ rank_ref[0], 0))],
            out_specs=pl.BlockSpec((rows, width), lambda i, rank_ref: (i, 0)),
        ),
        out_shape=jax.ShapeDtypeStruct(values.shape, values.dtype),
        name="reorder",
    )(rank, values)


def block_mask(segment_flat, block_start, block_stop):
    query_segment = segment_flat[block_start:block_stop]
    key_segment = segment_flat[:block_stop]
    query_slot = jnp.arange(block_start, block_stop, dtype=jnp.int32)
    key_slot = jnp.arange(0, block_stop, dtype=jnp.int32)
    return (query_segment[:, None] == key_segment[None, :]) & (
        key_slot[None, :] <= query_slot[:, None]
    )


def attend(segment_flat, queries, keys, values, block_size):
    out_pieces, total_pieces = [], []
    for start in range(0, SLOTS, block_size):
        stop = start + block_size
        allowed = block_mask(segment_flat, start, stop)
        scores = contract_last(queries[start:stop], keys[:stop])
        scores = jnp.where(allowed, scores, -1e30)
        row_max = jnp.max(scores, axis=-1, keepdims=True)
        expanded = jnp.exp(scores - row_max)
        row_total = jnp.sum(expanded, axis=-1, keepdims=True)
        probability = (expanded / row_total).astype(bf16)
        out_pieces.append(dot(probability, values[:stop]))
        total_pieces.append(row_max + jnp.log(row_total))
    return jnp.concatenate(out_pieces, axis=0), jnp.concatenate(total_pieces, axis=0)


def attend_back(segment_flat, queries, keys, values, grads, log_total, block_size):
    query_pieces = []
    key_grad = jnp.zeros(keys.shape, f32)
    value_grad = jnp.zeros(values.shape, f32)
    for start in range(0, SLOTS, block_size):
        stop = start + block_size
        allowed = block_mask(segment_flat, start, stop)
        scores = contract_last(queries[start:stop], keys[:stop])
        scores = jnp.where(allowed, scores, -1e30)
        probability = jnp.exp(scores - log_total[start:stop])
        prob_grad = contract_last(grads[start:stop], values[:stop])
        value_grad = value_grad.at[:stop].add(
            contract_first(probability.astype(bf16), grads[start:stop])
        )
        delta = jnp.sum(probability * prob_grad, axis=-1, keepdims=True)
        score_grad = (probability * (prob_grad - delta)).astype(bf16)
        query_pieces.append(dot(score_grad, keys[:stop]))
        key_grad = key_grad.at[:stop].add(contract_first(score_grad, queries[start:stop]))
    return jnp.concatenate(query_pieces, axis=0), key_grad, value_grad


def body(
    tokens,
    lengths,
    attention_gain,
    query_weight,
    key_weight,
    value_weight,
    output_weight,
    lambda_vectors,
    head_gain,
    feedforward_gain,
    gate_weight,
    up_weight,
    down_weight,
    cotangent,
):
    rows_here = tokens.shape[0]
    cores = lax.axis_size("tensor")
    groups = lax.axis_size("head") * cores
    group_rank = lax.axis_index("head") * cores + lax.axis_index("tensor")
    rank = group_rank.astype(jnp.int32).reshape(1)
    map_index = lax.axis_index("tensor")
    heads = query_weight.shape[1]
    width = query_weight.shape[3]
    value_half = value_weight.shape[2]
    value_width = value_half * cores
    shard_rows = query_weight.shape[0]
    quarter = rows_here * cores
    block_size = min(block_limit, SLOTS)

    weights = Chain(2)
    qkv_full = ring_gather(
        weights,
        jnp.concatenate(
            [
                query_weight.reshape(shard_rows, -1),
                key_weight.reshape(shard_rows, -1),
                value_weight.reshape(shard_rows, -1),
            ],
            axis=1,
        ),
        0,
    )
    output_full = ring_gather(weights, output_weight.reshape(-1, output_weight.shape[2]), 1)
    gate_full = ring_gather(weights, gate_weight, 0)
    up_full = ring_gather(weights, up_weight, 0)
    down_full = ring_gather(weights, down_weight, 1)

    tokens_wide = tokens.astype(f32)
    attention_scale = lax.rsqrt(jnp.mean(tokens_wide * tokens_wide, axis=-1, keepdims=True) + 1e-06)
    normed_all = gather_rows((tokens_wide * attention_scale * attention_gain).astype(bf16))

    segment, positions = slot_layout(lengths)
    segment_flat = segment.reshape(-1)
    valid_all = (segment_flat < 2).astype(f32)
    valid_here = lax.dynamic_slice_in_dim(valid_all, group_rank * rows_here, rows_here)[:, None]
    cosine_table, sine_table = rope_tables(positions.reshape(-1), width)
    head_start = lax.axis_index("head") * heads
    own_vectors = lax.dynamic_slice_in_dim(lambda_vectors, head_start, heads, 0)
    first_exp = jnp.exp(jnp.sum(own_vectors[:, 0] * own_vectors[:, 1], axis=-1))
    second_exp = jnp.exp(jnp.sum(own_vectors[:, 2] * own_vectors[:, 3], axis=-1))
    lambda_value = first_exp - second_exp + lambda_base
    coefficient = jnp.where(map_index == 0, jnp.ones_like(lambda_value), -lambda_value)
    own_gain = lax.dynamic_slice(
        head_gain, (head_start, map_index * value_half), (heads, value_half)
    ) * (1.0 - lambda_base)

    pre = dot(normed_all, qkv_full)
    queries, keys, values_own = rope_blocks(
        rank, pre, cosine_table, sine_table, heads, width, groups
    )
    values_other = flip(values_own, "tensor", 1)

    ffn_out_grad = valid_here * cotangent.astype(f32)
    ffn_grad_all = gather_rows(after(ffn_out_grad.astype(bf16), queries))

    def cols(array, head, size):
        return array[:, head * size : (head + 1) * size]

    values = [
        jnp.concatenate([cols(values_own, h, value_half), cols(values_other, h, value_half)], 1)
        for h in range(heads)
    ]
    maps_out, log_total = [], []
    for h in range(heads):
        out, total = attend(
            segment_flat, cols(queries, h, width), cols(keys, h, width), values[h], block_size
        )
        maps_out.append(out)
        log_total.append(total)
    scaled = [maps_out[h] * coefficient[h] for h in range(heads)]
    sent = flip(jnp.concatenate([s[:, value_half:] for s in scaled], 1), "tensor", 1)
    mixed = [scaled[h][:, :value_half] + cols(sent, h, value_half) for h in range(heads)]
    squares = jnp.concatenate([jnp.sum(m * m, axis=-1, keepdims=True) for m in mixed], 1)
    square_sum = squares + flip(squares, "tensor", 1)
    head_scale = lax.rsqrt(square_sum / value_width + 1e-05)
    head_out = reorder(
        rank,
        jnp.concatenate(
            [
                (mixed[h] * head_scale[:, h : h + 1] * own_gain[h][None]).astype(bf16)
                for h in range(heads)
            ],
            1,
        ),
        groups,
    )
    attention_here = scatter_rows(
        lambda m: dot(head_out[m * quarter : (m + 1) * quarter], output_full)
    )
    residual = tokens_wide + attention_here
    ffn_scale = lax.rsqrt(jnp.mean(residual * residual, axis=-1, keepdims=True) + 1e-06)
    ffn_all = gather_rows((residual * ffn_scale * feedforward_gain).astype(bf16))

    hidden_grad = contract_last(ffn_grad_all, down_full)
    gate_pre = dot(ffn_all, gate_full)
    upward = dot(ffn_all, up_full)
    sigmoid_gate = jax.nn.sigmoid(gate_pre)
    silu_gate = gate_pre * sigmoid_gate
    hidden = (silu_gate * upward).astype(bf16)
    gate_grad = (
        hidden_grad * upward * sigmoid_gate * (1.0 + gate_pre * (1.0 - sigmoid_gate))
    ).astype(bf16)
    up_grad = (hidden_grad * silu_gate).astype(bf16)

    def ffn_part(m):
        at = slice(m * quarter, (m + 1) * quarter)
        return contract_last(gate_grad[at], gate_full) + contract_last(up_grad[at], up_full)

    ffn_in_grad = scatter_rows(ffn_part)
    down_weight_grad = contract_first(hidden, ffn_grad_all).astype(bf16)
    gate_weight_grad = contract_first(ffn_all, gate_grad).astype(bf16)
    up_weight_grad = contract_first(ffn_all, up_grad).astype(bf16)
    grads = Chain(2)
    down_grad_out = ring_scatter(grads, down_weight_grad, 1)
    gate_grad_out = ring_scatter(grads, gate_weight_grad, 0)
    up_grad_out = ring_scatter(grads, up_weight_grad, 0)

    feedforward_gain_grad = jnp.sum(ffn_in_grad * residual * ffn_scale, axis=0)
    ffn_gained = ffn_in_grad * feedforward_gain
    residual_grad = (
        ffn_out_grad
        + ffn_scale * ffn_gained
        - residual * ffn_scale**3 * jnp.mean(ffn_gained * residual, axis=-1, keepdims=True)
    )
    attention_grad_all = gather_rows(residual_grad.astype(bf16))

    hidden_late = after(hidden, attention_grad_all)
    ffn_here = scatter_rows(
        lambda m: dot(hidden_late[m * quarter : (m + 1) * quarter], down_full)
    )
    block_output = (valid_here * (residual + ffn_here)).astype(bf16)

    head_out_grad = reorder(rank, contract_last(attention_grad_all, output_full), groups)
    output_weight_grad = contract_first(head_out, attention_grad_all).astype(bf16)
    output_grad_out = ring_scatter(grads, output_weight_grad, 1)

    out_grads = [cols(head_out_grad, h, value_half) for h in range(heads)]
    head_gain_part = jnp.stack(
        [
            jnp.sum(out_grads[h] * mixed[h] * head_scale[:, h : h + 1], axis=0)
            for h in range(heads)
        ]
    ) * (1.0 - lambda_base)
    weighted = [out_grads[h] * own_gain[h][None] for h in range(heads)]
    inner = jnp.concatenate(
        [jnp.sum(weighted[h] * mixed[h], axis=-1, keepdims=True) for h in range(heads)], 1
    )
    inner_sum = inner + flip(inner, "tensor", 1)
    slope = head_scale**3 * (inner_sum / value_width)
    mixed_grad_own = jnp.concatenate(
        [
            (head_scale[:, h : h + 1] * weighted[h] - mixed[h] * slope[:, h : h + 1]).astype(bf16)
            for h in range(heads)
        ],
        1,
    )
    mixed_grad_other = flip(mixed_grad_own, "tensor", 1)
    query_grads, key_grads, value_owns, value_others, lambda_parts = [], [], [], [], []
    for h in range(heads):
        mixed_grad = jnp.concatenate(
            [cols(mixed_grad_own, h, value_half), cols(mixed_grad_other, h, value_half)], 1
        ).astype(f32)
        lambda_parts.append(jnp.sum(mixed_grad * maps_out[h]))
        map_grad = (mixed_grad * coefficient[h]).astype(bf16)
        query_grad, key_grad, value_grad = attend_back(
            segment_flat,
            cols(queries, h, width),
            cols(keys, h, width),
            values[h],
            map_grad,
            log_total[h],
            block_size,
        )
        query_grads.append(query_grad)
        key_grads.append(key_grad)
        value_owns.append(value_grad[:, :value_half])
        value_others.append(value_grad[:, value_half:].astype(bf16))
    value_grad_own = jnp.concatenate(value_owns, 1) + flip(
        jnp.concatenate(value_others, 1), "tensor", 1
    ).astype(f32)
    lambda_grad = jnp.stack(lambda_parts) * jnp.where(map_index == 1, -1.0, 0.0)
    vector_grads = jnp.stack(
        [
            lambda_grad[:, None] * first_exp[:, None] * own_vectors[:, 1],
            lambda_grad[:, None] * first_exp[:, None] * own_vectors[:, 0],
            -lambda_grad[:, None] * second_exp[:, None] * own_vectors[:, 3],
            -lambda_grad[:, None] * second_exp[:, None] * own_vectors[:, 2],
        ],
        axis=1,
    )
    lambda_full = lax.dynamic_update_slice(
        jnp.zeros(lambda_vectors.shape, f32), vector_grads, (head_start, 0, 0)
    )
    gain_full = lax.dynamic_update_slice(
        jnp.zeros(head_gain.shape, f32), head_gain_part, (head_start, map_index * value_half)
    )
    qkv_grad = rope_back_blocks(
        rank,
        jnp.concatenate(query_grads, 1),
        jnp.concatenate(key_grads, 1),
        value_grad_own,
        cosine_table,
        sine_table,
        heads,
        width,
        groups,
    )
    qkv_weight_grad = contract_first(normed_all, qkv_grad).astype(bf16)
    qkv_grad_out = ring_scatter(grads, qkv_weight_grad, 0)
    normed_grad = scatter_rows(
        lambda m: contract_last(qkv_grad[m * quarter : (m + 1) * quarter], qkv_full)
    )
    attention_gain_grad = jnp.sum(normed_grad * tokens_wide * attention_scale, axis=0)
    attention_gained = normed_grad * attention_gain
    tokens_grad = (
        residual_grad
        + attention_scale * attention_gained
        - tokens_wide
        * attention_scale**3
        * jnp.mean(attention_gained * tokens_wide, axis=-1, keepdims=True)
    )
    axes = ("tensor", "head", "fsdp")
    early = total_over(
        jnp.concatenate(
            [
                feedforward_gain_grad.reshape(-1, 128),
                lambda_full.reshape(-1, 128),
                gain_full.reshape(-1, 128),
            ],
            0,
        ),
        axes,
    )
    late = total_over(attention_gain_grad.reshape(-1, 128), axes)
    first_at = feedforward_gain.size // 128
    second_at = first_at + lambda_vectors.size // 128
    part = heads * width
    return (
        block_output,
        tokens_grad,
        late.reshape(-1),
        qkv_grad_out[:, :part].reshape(query_weight.shape),
        qkv_grad_out[:, part : 2 * part].reshape(key_weight.shape),
        qkv_grad_out[:, 2 * part :].reshape(value_weight.shape),
        output_grad_out.reshape(output_weight.shape),
        early[first_at:second_at].reshape(lambda_vectors.shape),
        early[second_at:].reshape(head_gain.shape),
        early[:first_at].reshape(-1),
        gate_grad_out,
        up_grad_out,
        down_grad_out,
    )


def solution(mesh):
    placed = (
        P(("fsdp", "head", "tensor"), None),
        P("fsdp", None),
        P(),
        P("fsdp", "head", "tensor", None),
        P("fsdp", "head", "tensor", None),
        P("fsdp", "head", "tensor"),
        P("head", "tensor", "fsdp"),
        P(),
        P(),
        P(),
        P("fsdp", ("head", "tensor")),
        P("fsdp", ("head", "tensor")),
        P(("head", "tensor"), "fsdp"),
        P(("fsdp", "head", "tensor"), None),
    )
    return jax.shard_map(
        body,
        mesh=mesh,
        in_specs=placed,
        out_specs=(
            P(("fsdp", "head", "tensor"), None),
            P(("fsdp", "head", "tensor"), None),
            P(),
            P("fsdp", "head", "tensor", None),
            P("fsdp", "head", "tensor", None),
            P("fsdp", "head", "tensor"),
            P("head", "tensor", "fsdp"),
            P(),
            P(),
            P(),
            P("fsdp", ("head", "tensor")),
            P("fsdp", ("head", "tensor")),
            P(("head", "tensor"), "fsdp"),
        ),
        check_vma=False,
    )
```
